256 devices in a mesh: member: 16 (over x_lo, z), lat: 8 (over y, core), lon: 2 (over x_hi).
Axes of the slice: x: 4 (x_hi: 2, x_lo: 2; x = x_hi * 2 + x_lo), y: 4, z: 8, core: 2. Of those that a mesh axis runs over, the one named last changes fastest.
Arguments:
- state: float32 [32, 5, 2, 256, 1024], P('member', None, None, 'lat', 'lon'), may hold values from -4 to 4
- kick: float32 [32, 5, 2, 256, 1024], P('member', None, None, 'lat', 'lon'), may hold values from -3 to 3
- forcing: float32 [5, 2, 256, 1024], P(None, None, 'lat', 'lon'), may hold values from -4 to 4
- coupling: float32 [2, 5, 5], replicated, may hold values from -3 to 3
- clone_src: int32 [32], replicated, may hold values from 0 to 31, as said below
Outputs:
- advanced: float32 [32, 5, 2, 256, 1024], P('member', None, None, 'lat', 'lon')
The draws below stay inside these ranges and needn't reach their ends.
Inputs may be any that keep to these rules, and one draw needn't show every extreme that they name: `clone_src`: entry m equals m for a member that is kept; a replaced member names a member that is kept.
All inputs are finite; a program needn't handle non-finite values.
Results may differ from the reference program's by a relative error of at most 0.00012.
Values sent between devices are 32-bit elements; how exact they have to be, the bound alone decides.
A program may use at most 128 MiB of HBM per device.

```python
import jax
import jax.numpy as jnp
from jax import lax

VARS = 5
LEV = 2
STEPS = 4
MEM_DEV = 2
MEMBERS = 32
NLAT = 256
NLON = 1024


def draw_clone_src(key, part):
    keys = jax.random.split(key, 5)
    order = jax.random.permutation(keys[0], MEMBERS).astype(jnp.int32)
    cutoff = jax.random.randint(keys[1], (), 1, MEMBERS // 2 + 1).astype(jnp.int32)
    places = jnp.argsort(order, stable=True).astype(jnp.int32)
    replaced = places < cutoff
    first = jax.random.randint(keys[2], (MEMBERS,), 0, MEMBERS).astype(jnp.int32)
    second = jax.random.randint(keys[3], (MEMBERS,), 0, MEMBERS).astype(jnp.int32)
    ranks = jnp.minimum(first, second) % (MEMBERS - cutoff)
    source = jnp.take(order, cutoff + ranks)
    result = jnp.where(replaced, source, jnp.arange(MEMBERS, dtype=jnp.int32)).astype(jnp.int32)
    groups = MEMBERS // MEM_DEV
    anchor = jax.random.randint(keys[4], (), 0, groups).astype(jnp.int32)
    giver = (anchor * MEM_DEV).astype(jnp.int32)
    taker = ((anchor + 1) % groups * MEM_DEV + (MEM_DEV - 1)).astype(jnp.int32)
    result = jnp.where(result == taker, giver, result).astype(jnp.int32)
    result = result.at[giver].set(giver)
    result = result.at[taker].set(giver)
    return result.astype(jnp.int32)


def block_scale(key, shape, cuts, low, high):
    def one(axis_at, blocks):
        steps = jax.random.uniform(jax.random.fold_in(jax.random.fold_in(key, 6), axis_at), (blocks,), jnp.float32, low / len(cuts), high / len(cuts))
        return jnp.repeat(jnp.exp(steps), shape[axis_at] // blocks).reshape((-1,) + (1,) * (len(shape) - axis_at - 1))

    loudness = one(*cuts[0])
    for cut in cuts[1:]:
        loudness = loudness * one(*cut)
    return loudness


def bell_draw(own_key, extent, scale, most, cuts=(), kind=jnp.bfloat16):
    entries = scale * jax.random.normal(own_key, extent, jnp.float32)
    if cuts:
        entries = entries * block_scale(own_key, extent, cuts, -0.22, 0.18)
    return jnp.clip(entries, -most, most).astype(kind)


def setup_inputs(seed: int = 0) -> dict:
    seeds = jax.random.split(jax.random.key(seed), 6)
    state = bell_draw(seeds[0], (MEMBERS, VARS, LEV, NLAT, NLON), 1.0, 4.0, ((0, 16), (3, 8), (4, 2)), jnp.float32)
    kick = bell_draw(seeds[1], (MEMBERS, VARS, LEV, NLAT, NLON), 0.3, 3.0, ((0, 16), (3, 8), (4, 2)), jnp.float32)
    forcing = bell_draw(seeds[2], (VARS, LEV, NLAT, NLON), 1.0, 4.0, ((2, 8), (3, 2)), jnp.float32)
    coupling = bell_draw(seeds[3], (LEV, VARS, VARS), 0.3, 3.0, (), jnp.float32)
    clone_src = draw_clone_src(jax.random.fold_in(seeds[5], 71), 0)
    return {"state": state, "kick": kick, "forcing": forcing, "coupling": coupling, "clone_src": clone_src}


def advance(padded, forcing_c, coupling):
    h = padded.shape[3] - 4
    w = padded.shape[4] - 4

    def part(di, dj):
        return padded[:, :, :, 2 + di:2 + di + h, 2 + dj:2 + dj + w]

    centre = part(0, 0)
    along_x = (8.0 * (part(0, 1) - part(0, -1)) - (part(0, 2) - part(0, -2))) / 12.0
    along_y = (8.0 * (part(1, 0) - part(-1, 0)) - (part(2, 0) - part(-2, 0))) / 12.0
    near = part(0, 1) + part(0, -1) + part(1, 0) + part(-1, 0)
    far_sum = part(0, 2) + part(0, -2) + part(2, 0) + part(-2, 0)
    laplace = (16.0 * near - far_sum - 60.0 * centre) / 12.0
    wind_u = centre[:, 0:1]
    wind_v = centre[:, 1:2]
    mixed = jnp.einsum("kvw,mwkij->mvkij", coupling, centre, precision=lax.Precision.HIGHEST)
    return centre + (-0.05 * (wind_u * along_x + wind_v * along_y) + 0.05 * laplace + 0.25 * mixed + 0.1 * forcing_c)


def evolve(member, forcing, coupling):
    field = member[None]
    for step in range(STEPS):
        padded = jnp.pad(field, ((0, 0), (0, 0), (0, 0), (0, 0), (2, 2)), mode="wrap")
        padded = jnp.pad(padded, ((0, 0), (0, 0), (0, 0), (2, 2), (0, 0)))
        field = advance(padded, forcing, coupling)
    return field[0]


def reference(state, kick, forcing, coupling, clone_src):
    start = jnp.take(state, clone_src, axis=0) + kick
    return lax.map(lambda member: evolve(member, forcing, coupling), start)
```

```python
import functools

import jax
import jax.numpy as jnp
from jax import lax
from jax.experimental import pallas as pl
from jax.experimental.pallas import tpu as pltpu
from jax.sharding import PartitionSpec as P

STEPS = 4
HALO = 8
MESH = pl.DeviceIdType.MESH


def roll(values, shift):
    return pltpu.roll(values, shift % values.shape[-1], axis=values.ndim - 1)


def exchange_kernel(
    chunks, clone, state, kick, forcing, e_ref, f_ref,
    comb, outgoing, pack, packf, landed, landedf,
    load_sem, send1, recv1, send2, recv2, own_sem, edge_send, edge_recv, *pools,
):
    n = lax.axis_size("member")
    nlat = lax.axis_size("lat")
    me = lax.axis_index("member")
    lat = lax.axis_index("lat")
    lon = lax.axis_index("lon")
    planes = state.shape[1]
    per_chunk = planes // chunks
    up = lax.rem(lat + nlat - 1, nlat)
    down = lax.rem(lat + 1, nlat)
    across = 1 - lon

    load = pltpu.make_async_copy(state, comb.at[0:2], load_sem)
    load.start()

    barrier = pltpu.get_barrier_semaphore()

    def greet(r, _):
        pl.semaphore_signal(barrier, 1, device_id={"member": lax.rem(me + r, n)}, device_id_type=MESH)
        return 0

    lax.fori_loop(1, n, greet, 0)
    for peer in (
        {"lat": up}, {"lat": down}, {"lon": across},
        {"lat": up, "lon": across}, {"lat": down, "lon": across},
    ):
        pl.semaphore_signal(barrier, 1, device_id=peer, device_id_type=MESH)
    load.wait()
    pl.semaphore_wait(barrier, n - 1 + 5)

    def window(piece):
        rows = pl.ds(pl.multiple_of(piece // 4 * 8, 8), 8)
        cols = pl.ds(pl.multiple_of(lax.rem(piece, 4) * 128, 128), 128)
        return rows, cols

    def spread(k, r):
        peer = lax.rem(me + r, n)
        rows, cols = window(peer)
        some = pl.ds(k * per_chunk, per_chunk)
        return pltpu.make_async_remote_copy(
            comb.at[0:2, some, rows, cols], pools[k].at[me],
            send1.at[k, r], recv1.at[k, r], device_id={"member": peer}, device_id_type=MESH,
        )

    def collect(k, r):
        peer = lax.rem(me + r, n)
        rows, cols = window(me)
        some = pl.ds(k * per_chunk, per_chunk)
        return pltpu.make_async_remote_copy(
            outgoing.at[peer, :, some], comb.at[2:4, some, rows, cols],
            send2.at[k, r], recv2.at[k, r], device_id={"member": peer}, device_id_type=MESH,
        )

    for k in range(chunks):
        lax.fori_loop(1, n, lambda r, c: (spread(k, r).start(), c)[1], 0)
    my_rows, my_cols = window(me)
    owns = [
        pltpu.make_async_copy(
            comb.at[0:2, k * per_chunk : (k + 1) * per_chunk, my_rows, my_cols], pools[k].at[me], own_sem.at[k]
        )
        for k in range(chunks)
    ]
    for own in owns:
        own.start()

    lane = lax.broadcasted_iota(jnp.int32, (32, 128), 1)

    def edge_copies(rim, packed, arrived, base):
        hops = (
            (rim.at[:, 0:4, 8:16], rim.at[:, 0:4, 40:48], {"lat": up}),
            (rim.at[:, 0:4, 32:40], rim.at[:, 0:4, 0:8], {"lat": down}),
            (packed, arrived.at[:, 8:40], {"lon": across}),
            (packed.at[:, 0:8], arrived.at[:, 40:48], {"lat": up, "lon": across}),
            (packed.at[:, 24:32], arrived.at[:, 0:8], {"lat": down, "lon": across}),
        )
        return [
            pltpu.make_async_remote_copy(
                source, target, edge_send.at[base + i], edge_recv.at[base + i],
                device_id=peer, device_id_type=MESH,
            )
            for i, (source, target, peer) in enumerate(hops)
        ]

    def pack_edges(rim, packed, count):
        for group in range((count + 7) // 8):
            total = None
            for slot in range(min(8, count - 8 * group)):
                p = 8 * group + slot
                tile = jnp.where(lane < 64, rim[p, 0, 8:40], rim[p, 3, 8:40])
                tile = roll(tile, 16 * slot)
                if total is None:
                    total = tile
                else:
                    first = 16 * slot - 8
                    total = jnp.where((lane >= first) & (lane < first + 16), tile, total)
            packed[group] = total

    def unpack_edges(rim, arrived, count):
        for p in range(count):
            rim[p, 4] = roll(arrived[p // 8], -16 * (p % 8))

    def clear_outside(rim):
        @pl.when(lat == 0)
        def _():
            rim[:, :, 0:8] = jnp.zeros((rim.shape[0], 5, 8, 128), jnp.float32)

        @pl.when(lat == nlat - 1)
        def _():
            rim[:, :, 40:48] = jnp.zeros((rim.shape[0], 5, 8, 128), jnp.float32)

    for ct in range(4):
        f_ref[:, ct, 8:40] = forcing[:, :, ct * 128 : ct * 128 + 128]
    pack_edges(f_ref, packf, planes)
    f_copies = edge_copies(f_ref, packf, landedf, 5)
    for copy in f_copies:
        copy.start()

    for k in range(chunks):
        owns[k].wait()
        lax.fori_loop(1, n, lambda r, c: (spread(k, r).wait_recv(), c)[1], 0)
        some = pl.ds(k * per_chunk, per_chunk)

        def choose(d, c):
            for j in range(2):
                source = clone[2 * d + j]
                outgoing[d, j, some] = pools[k][source // 2, lax.rem(source, 2)]
            return c

        lax.fori_loop(0, n, choose, 0)
        lax.fori_loop(1, n, lambda r, c: (collect(k, r).start(), c)[1], 0)
    mine = pltpu.make_async_copy(outgoing.at[me], comb.at[2:4, :, my_rows, my_cols], own_sem.at[0])
    mine.start()
    for k in range(chunks):
        lax.fori_loop(1, n, lambda r, c: (spread(k, r).wait_send(), c)[1], 0)
    mine.wait()
    for k in range(chunks):
        lax.fori_loop(1, n, lambda r, c: (collect(k, r).wait_recv(), c)[1], 0)

    def begin(p, c):
        for j in range(2):
            source = clone[2 * me + j]
            pick = jnp.where(source // 2 == me, lax.rem(source, 2), 2 + j)
            for ct in range(4):
                cols = slice(ct * 128, ct * 128 + 128)
                e_ref[j * planes + p, ct, 8:40] = comb[pick, p, :, cols] + kick[j, p, :, cols]
        return c

    lax.fori_loop(0, planes, begin, 0)
    pack_edges(e_ref, pack, 2 * planes)
    e_copies = edge_copies(e_ref, pack, landed, 0)
    for copy in e_copies:
        copy.start()
    for copy in f_copies:
        copy.wait()
    unpack_edges(f_ref, landedf, planes)
    for k in range(chunks):
        lax.fori_loop(1, n, lambda r, c: (collect(k, r).wait_send(), c)[1], 0)
    for copy in e_copies:
        copy.wait()
    unpack_edges(e_ref, landed, 2 * planes)
    clear_outside(e_ref)


def step_kernel(coupling, edge, e_ref, f_ref, out_ref, work_a, work_b, mix):
    for k in range(2):
        for v in range(5):
            for w in range(5):
                scaled = 0.25 * coupling[k, v, w]
                mix[k, v, w] = scaled + 0.75 if v == w else scaled
    lane = lax.broadcasted_iota(jnp.int32, (8, 128), 1)
    row_at = lax.broadcasted_iota(jnp.int32, (8, 128), 0)
    low, high = edge[0], edge[1]
    one12 = 1.0 / 12.0

    def sweep(source, target, starts, last):
        tiles = 4 if last else 5

        def block(combo, row):
            m, k = combo // 2, lax.rem(combo, 2)
            base = m * 10 + k
            centre = [[source[base + 2 * v, c, pl.ds(row, 8)] for c in range(5)] for v in range(5)]
            for c in range(tiles):
                u = centre[0][c]
                w = centre[1][c]
                u8, u1 = u * (-0.4 * one12), u * (0.05 * one12)
                v8, v1 = w * (-0.4 * one12), w * (0.05 * one12)
                for v in range(5):
                    here = centre[v]
                    before, after = here[(c + 4) % 5], here[(c + 1) % 5]
                    w1 = jnp.where(lane < 1, roll(before, 1), roll(here[c], 1))
                    w2 = jnp.where(lane < 2, roll(before, 2), roll(here[c], 2))
                    e1 = jnp.where(lane >= 127, roll(after, -1), roll(here[c], -1))
                    e2 = jnp.where(lane >= 126, roll(after, -2), roll(here[c], -2))
                    p = base + 2 * v
                    n1 = source[p, c, pl.ds(row - 1, 8)]
                    n2 = source[p, c, pl.ds(row - 2, 8)]
                    s1 = source[p, c, pl.ds(row + 1, 8)]
                    s2 = source[p, c, pl.ds(row + 2, 8)]
                    near = (e1 + w1) + (s1 + n1)
                    far = (e2 + w2) + (s2 + n2)
                    total = u8 * (e1 - w1) + u1 * (e2 - w2) + v8 * (s1 - n1) + v1 * (s2 - n2)
                    total = total + (near * (0.8 * one12) - far * (0.05 * one12))
                    total = total + 0.1 * f_ref[2 * v + k, c, pl.ds(row, 8)]
                    for q in range(5):
                        total = total + mix[k, v, q] * centre[q][c]
                    if last:
                        out_ref[m, 2 * v + k, pl.ds(row - HALO, 8), c * 128 : c * 128 + 128] = total
                    else:
                        inside = (row_at + row >= low) & (row_at + row < high)
                        target[p, c, pl.ds(row, 8)] = jnp.where(inside, total, 0.0)

        def combos(combo, _):
            for row in starts:
                block(combo, row)
            return 0

        lax.fori_loop(0, 4, combos, 0)

    sweep(e_ref, work_a, (2, 10, 18, 26, 34, 38), False)
    sweep(work_a, work_b, (4, 12, 20, 28, 36), False)
    sweep(work_b, work_a, (6, 14, 22, 30, 34), False)
    sweep(work_a, None, (8, 16, 24, 32), True)


def shards(state, kick, forcing, coupling, clone_src):
    shape = state.shape
    planes = shape[1] * shape[2]
    flat = (shape[0], planes, shape[3], shape[4])
    n = lax.axis_size("member")
    chunks = 2
    f32 = jnp.float32
    vmem = pl.BlockSpec(memory_space=pltpu.VMEM)
    smem = pl.BlockSpec(memory_space=pltpu.SMEM)
    dma = pltpu.SemaphoreType.DMA
    e, f = pl.pallas_call(
        functools.partial(exchange_kernel, chunks),
        out_shape=(
            jax.ShapeDtypeStruct((2 * planes, 5, 48, 128), f32),
            jax.ShapeDtypeStruct((planes, 5, 48, 128), f32),
        ),
        in_specs=[smem, pl.BlockSpec(memory_space=pl.ANY), vmem, vmem],
        out_specs=(vmem, vmem),
        scratch_shapes=[
            pltpu.VMEM((4,) + flat[1:], f32),
            pltpu.VMEM((n, 2, planes, 8, 128), f32),
            pltpu.VMEM((3, 32, 128), f32),
            pltpu.VMEM((2, 32, 128), f32),
            pltpu.VMEM((3, 48, 128), f32),
            pltpu.VMEM((2, 48, 128), f32),
            dma(()),
            dma((chunks, n)), dma((chunks, n)), dma((chunks, n)), dma((chunks, n)),
            dma((chunks,)), dma((10,)), dma((10,)),
        ]
        + [pltpu.VMEM((n, 2, planes // chunks, 8, 128), f32)] * chunks,
        compiler_params=pltpu.CompilerParams(collective_id=0, has_side_effects=True),
        name="exchange",
    )(clone_src, state.reshape(flat), kick.reshape(flat), forcing.reshape(flat[1:]))
    lat, nlat = lax.axis_index("lat"), lax.axis_size("lat")
    edge = jnp.stack([jnp.where(lat == 0, HALO, 0), jnp.where(lat == nlat - 1, 40, 48)]).astype(jnp.int32)
    out = pl.pallas_call(
        step_kernel,
        out_shape=jax.ShapeDtypeStruct(flat, f32),
        in_specs=[smem, smem, vmem, vmem],
        out_specs=vmem,
        scratch_shapes=[
            pltpu.VMEM((2 * planes, 5, 48, 128), f32),
            pltpu.VMEM((2 * planes, 5, 48, 128), f32),
            pltpu.SMEM((2, 5, 5), f32),
        ],
        name="steps",
    )(coupling, edge, e, f)
    return out.reshape(shape)


def solution(mesh):
    block = P("member", None, None, "lat", "lon")
    in_specs = (block, block, P(None, None, "lat", "lon"), P(), P())
    return jax.shard_map(shards, mesh=mesh, in_specs=in_specs, out_specs=block, check_vma=False)
```

```python
import functools

import jax
import jax.numpy as jnp
from jax import lax
from jax.experimental import pallas as pl
from jax.experimental.pallas import tpu as pltpu
from jax.sharding import PartitionSpec as P

HALO = 8
WIDE = 112
MESH = pl.DeviceIdType.MESH


def roll(values, shift):
    if isinstance(shift, int):
        shift = shift % 128
    return pltpu.roll(values, shift, axis=values.ndim - 1)


def kernel(
    nsrc, ndst, tab, clone, state, kick_hbm, forcing_hbm, coupling, out_ref,
    comb0, comb1, kick, forcing, picked, pool0, pool1, outgoing0, outgoing1,
    e0, e1, f_ref, work_a, work_b, pack0, pack1, packf, landed0, landed1, landedf, mix,
    load_sem, send1, recv1, send2, recv2, own_sem, edge_send, edge_recv,
):
    comb, pool, outgoing = (comb0, comb1), (pool0, pool1), (outgoing0, outgoing1)
    rim, pack, landed = (e0, e1), (pack0, pack1), (landed0, landed1)
    n = lax.axis_size("member")
    nlat = lax.axis_size("lat")
    me = lax.axis_index("member")
    lat = lax.axis_index("lat")
    across = 1 - lax.axis_index("lon")
    up = lax.rem(lat + nlat - 1, nlat)
    down = lax.rem(lat + 1, nlat)

    loads = [pltpu.make_async_copy(state.at[:, :, k], comb[k].at[0:2], load_sem.at[k]) for k in range(2)]
    loads.append(pltpu.make_async_copy(forcing_hbm, forcing, load_sem.at[2]))
    loads.append(pltpu.make_async_copy(kick_hbm, kick, load_sem.at[3]))
    for load in loads:
        load.start()

    barrier = pltpu.get_barrier_semaphore()

    def greet(r, _):
        pl.semaphore_signal(barrier, 1, device_id={"member": lax.rem(me + r, n)}, device_id_type=MESH)
        return 0

    lax.fori_loop(1, n, greet, 0)
    for peer in (
        {"lat": up}, {"lat": down}, {"lon": across},
        {"lat": up, "lon": across}, {"lat": down, "lon": across},
    ):
        pl.semaphore_signal(barrier, 1, device_id=peer, device_id_type=MESH)
    loads[0].wait()
    loads[1].wait()
    if nsrc == 1:
        first = tab[me] == 0

        def pick_one(v, c):
            for k in range(2):
                picked[0, v, k] = jnp.where(first, comb[k][0, v], comb[k][1, v])
            return c

        lax.fori_loop(0, 5, pick_one, 0)
    pl.semaphore_wait(barrier, n - 1 + 5)

    def window(piece):
        rows = pl.ds(pl.multiple_of(piece // 4 * 8, 8), 8)
        cols = pl.ds(pl.multiple_of(lax.rem(piece, 4) * 128, 128), 128)
        return rows, cols

    def given(k, rows, cols):
        if nsrc == 1:
            return picked.at[:, :, k, rows, cols]
        return comb[k].at[0:2, :, rows, cols]

    def spread(k, r):
        peer = lax.rem(me + r, n)
        return pltpu.make_async_remote_copy(
            given(k, *window(peer)), pool[k].at[me],
            send1.at[k, r], recv1.at[k, r], device_id={"member": peer}, device_id_type=MESH,
        )

    my_rows, my_cols = window(me)

    def collect(k, r):
        peer = lax.rem(me + r, n)
        return pltpu.make_async_remote_copy(
            outgoing[k].at[peer], comb[k].at[2 : 2 + ndst, :, my_rows, my_cols],
            send2.at[k, r], recv2.at[k, r], device_id={"member": peer}, device_id_type=MESH,
        )

    def peers(action):
        lax.fori_loop(1, n, lambda r, c: (action(r), c)[1], 0)

    for k in range(2):
        peers(lambda r: spread(k, r).start())
    owns = [pltpu.make_async_copy(given(k, my_rows, my_cols), pool[k].at[me], own_sem.at[k]) for k in range(2)]
    for own in owns:
        own.start()

    lane = lax.broadcasted_iota(jnp.int32, (32, 128), 1)

    def edge_copies(source, packed, arrived, base):
        hops = (
            (source.at[:, :, 8:16], source.at[:, :, 40:48], {"lat": up}),
            (source.at[:, :, 32:40], source.at[:, :, 0:8], {"lat": down}),
            (packed, arrived.at[:, 8:40], {"lon": across}),
            (packed.at[:, 0:8], arrived.at[:, 40:48], {"lat": up, "lon": across}),
            (packed.at[:, 24:32], arrived.at[:, 0:8], {"lat": down, "lon": across}),
        )
        return [
            pltpu.make_async_remote_copy(
                a, b, edge_send.at[base + i], edge_recv.at[base + i], device_id=peer, device_id_type=MESH
            )
            for i, (a, b, peer) in enumerate(hops)
        ]

    def lay_out(p, tiles, target, packed):
        target[p, 0, 8:40] = roll(tiles[0], 8)
        for c in range(1, 4):
            target[p, c, 8:40] = jnp.where(
                lane < 8 + 16 * c, roll(tiles[c - 1], 8 + 16 * c), roll(tiles[c], 8 + 16 * c)
            )
        target[p, 4, 8:40] = roll(tiles[3], 72)
        slot = lax.rem(p, 8)
        tile = roll(jnp.where(lane < 64, tiles[0], tiles[3]), 16 * slot)
        ours = lax.rem(lane + 8 + 128 - 16 * slot, 128) < 16
        packed[p // 8] = jnp.where(ours, tile, packed[p // 8])

    lane_tall = lax.broadcasted_iota(jnp.int32, (48, 128), 1)

    def add_columns(target, arrived):
        def one(p, c):
            turn = 128 - 16 * lax.rem(p, 8)
            source = arrived[p // 8]
            target[p, 0] = jnp.where(lane_tall < 8, roll(source, lax.rem(turn + 8, 128)), target[p, 0])
            target[p, 4] = jnp.where(lane_tall >= 72, roll(source, lax.rem(turn + 72, 128)), target[p, 4])
            return c

        lax.fori_loop(0, 10, one, 0)

    def clear_outside(target):
        @pl.when(lat == 0)
        def _():
            target[:, :, 0:8] = jnp.zeros((10, 5, 8, 128), jnp.float32)

        @pl.when(lat == nlat - 1)
        def _():
            target[:, :, 40:48] = jnp.zeros((10, 5, 8, 128), jnp.float32)

    def columns(ref, *index):
        return [ref[index + (slice(None), slice(t * 128, t * 128 + 128))] for t in range(4)]

    for k in range(2):
        pack[k][...] = jnp.zeros(pack[k].shape, jnp.float32)
    packf[...] = jnp.zeros(packf.shape, jnp.float32)
    loads[2].wait()

    def lay_forcing(p, c):
        tiles = columns(forcing, lax.rem(p, 5), p // 5)
        lay_out(p, [0.1 * t for t in tiles], f_ref, packf)
        return c

    lax.fori_loop(0, 10, lay_forcing, 0)
    f_copies = edge_copies(f_ref, packf, landedf, 10)
    for copy in f_copies:
        copy.start()

    for k in range(2):
        for v in range(5):
            table = coupling[v]
            for w in range(5):
                scaled = 0.25 * table[k, w]
                mix[k, v, w] = scaled + 0.75 if v == w else scaled

    for k in range(2):
        owns[k].wait()
        peers(lambda r: spread(k, r).wait_recv())

        def choose(d, c):
            for j in range(ndst):
                source = clone[2 * d + j] if ndst == 2 else clone[2 * d + tab[16 + d]]
                place = lax.rem(source, 2) if nsrc == 2 else 0
                outgoing[k][d, j] = pool[k][source // 2, place]
            return c

        lax.fori_loop(0, n, choose, 0)
        peers(lambda r: collect(k, r).start())
        mine = pltpu.make_async_copy(
            outgoing[k].at[me], comb[k].at[2 : 2 + ndst, :, my_rows, my_cols], own_sem.at[k]
        )
        mine.start()
        owns[k] = mine

    loads[3].wait()
    for k in range(2):
        peers(lambda r: spread(k, r).wait_send())
    for copy in f_copies:
        copy.wait()
    add_columns(f_ref, landedf)

    row_at = lax.broadcasted_iota(jnp.int32, (8, 128), 0)
    low = jnp.where(lat == 0, HALO, 0)
    high = jnp.where(lat == nlat - 1, 40, 48)
    near, far, first, second = 0.8 / 12.0, 0.05 / 12.0, 0.4 / 12.0, 0.05 / 12.0

    def sweep(k, source, target, starts):
        def tile(it, carry):
            m, c = it // 5, lax.rem(it, 5)
            for row in starts:
                centre = [source[5 * m + v, c, row : row + 8] for v in range(5)]
                u1, v1 = centre[0] * first, centre[1] * first
                u2, v2 = centre[0] * second, centre[1] * second
                ce1, cw1, ce2, cw2 = near - u1, near + u1, u2 - far, -far - u2
                cs1, cn1, cs2, cn2 = near - v1, near + v1, v2 - far, -far - v2
                for v in range(5):
                    p = 5 * m + v
                    here = centre[v]
                    along = cw1 * roll(here, 1) + ce1 * roll(here, -1)
                    along = along + (cw2 * roll(here, 2) + ce2 * roll(here, -2))
                    cross = cn1 * source[p, c, row - 1 : row + 7] + cs1 * source[p, c, row + 1 : row + 9]
                    cross = cross + (
                        cn2 * source[p, c, row - 2 : row + 6] + cs2 * source[p, c, row + 2 : row + 10]
                    )
                    rest = f_ref[5 * k + v, c, row : row + 8] + mix[k, v, 0] * centre[0]
                    for q in range(1, 5):
                        rest = rest + mix[k, v, q] * centre[q]
                    total = (along + cross) + rest
                    if row < 8 or row > 32:
                        inside = (row_at + row >= low) & (row_at + row < high)
                        total = jnp.where(inside, total, 0.0)
                    target[p, c, row : row + 8] = total
            return carry

        lax.fori_loop(0, 10, tile, 0)

    for k in range(2):
        owns[k].wait()
        peers(lambda r: collect(k, r).wait_recv())

        def begin(p, c):
            m, v = p // 5, lax.rem(p, 5)
            source = clone[2 * me + m]
            other = 2 + m if ndst == 2 else 2
            pick = jnp.where(source // 2 == me, lax.rem(source, 2), other)
            taken = columns(comb[k], pick, v)
            kicks = columns(kick, m, v, k)
            lay_out(p, [a + b for a, b in zip(taken, kicks)], rim[k], pack[k])
            return c

        lax.fori_loop(0, 10, begin, 0)
        copies = edge_copies(rim[k], pack[k], landed[k], 5 * k)
        for copy in copies:
            copy.start()
        for copy in copies:
            copy.wait()
        add_columns(rim[k], landed[k])
        clear_outside(rim[k])
        sweep(k, rim[k], work_a, (2, 10, 18, 26, 34, 38))
        sweep(k, work_a, work_b, (4, 12, 20, 28, 36))
        sweep(k, work_b, work_a, (6, 14, 22, 30, 34))
        sweep(k, work_a, work_b, (8, 16, 24, 32))

        def finish(p, c):
            m, v = p // 5, lax.rem(p, 5)
            turned = [roll(work_b[p, t, 8:40], -8 - 16 * t) for t in range(5)]
            for t in range(4):
                out_ref[m, v, k, :, t * 128 : t * 128 + 128] = jnp.where(
                    lane < WIDE - 16 * t, turned[t], turned[t + 1]
                )
            return c

        lax.fori_loop(0, 10, finish, 0)

    for k in range(2):
        peers(lambda r: collect(k, r).wait_send())


def run(nsrc, ndst, tab, clone_src, state, kick, forcing, coupling):
    n = lax.axis_size("member")
    f32 = jnp.float32
    vmem = pl.BlockSpec(memory_space=pltpu.VMEM)
    smem = pl.BlockSpec(memory_space=pltpu.SMEM)
    hbm = pl.BlockSpec(memory_space=pl.ANY)
    dma = pltpu.SemaphoreType.DMA
    member = state.shape[1:]
    level = (member[0],) + member[2:]
    padded = pltpu.VMEM((10, 5, 48, 128), f32)
    packed = pltpu.VMEM((2, 32, 128), f32)
    arrived = pltpu.VMEM((2, 48, 128), f32)
    return pl.pallas_call(
        functools.partial(kernel, nsrc, ndst),
        out_shape=jax.ShapeDtypeStruct(state.shape, f32),
        in_specs=[smem, smem, hbm, hbm, hbm, vmem],
        out_specs=vmem,
        scratch_shapes=[
            pltpu.VMEM((2 + ndst,) + level, f32), pltpu.VMEM((2 + ndst,) + level, f32),
            pltpu.VMEM(state.shape, f32), pltpu.VMEM(member, f32), pltpu.VMEM((1,) + member, f32),
            pltpu.VMEM((n, nsrc, 5, 8, 128), f32), pltpu.VMEM((n, nsrc, 5, 8, 128), f32),
            pltpu.VMEM((n, ndst, 5, 8, 128), f32), pltpu.VMEM((n, ndst, 5, 8, 128), f32),
            padded, padded, padded, padded, padded,
            packed, packed, packed, arrived, arrived, arrived,
            pltpu.SMEM((2, 5, 5), f32),
            dma((4,)), dma((2, n)), dma((2, n)), dma((2, n)), dma((2, n)),
            dma((2,)), dma((15,)), dma((15,)),
        ],
        compiler_params=pltpu.CompilerParams(collective_id=2 * nsrc + ndst, has_side_effects=True),
        name=f"advance_{nsrc}_{ndst}",
    )(tab, clone_src, state, kick, forcing, coupling.transpose(1, 0, 2))


def shards(state, kick, forcing, coupling, clone_src):
    return run(2, 2, clone_src, clone_src, state, kick, forcing, coupling)


def solution(mesh):
    block = P("member", None, None, "lat", "lon")
    in_specs = (block, block, P(None, None, "lat", "lon"), P(), P())
    return jax.shard_map(shards, mesh=mesh, in_specs=in_specs, out_specs=block, check_vma=False)
```

```python
import functools

import jax
import jax.numpy as jnp
from jax import lax
from jax.experimental import pallas as pl
from jax.experimental.pallas import tpu as pltpu
from jax.sharding import PartitionSpec as P

HALO = 8
WIDE = 112
MESH = pl.DeviceIdType.MESH


def roll(values, shift):
    if isinstance(shift, int):
        shift = shift % 128
    return pltpu.roll(values, shift, axis=values.ndim - 1)


def kernel(
    nsrc, ndst, tab, clone, state, kick_hbm, forcing_hbm, coupling, out_ref,
    comb0, comb1, kick, forcing, picked, pool0, pool1, outgoing0, outgoing1,
    e0, e1, f_ref, work_a, work_b, pack0, pack1, packf, landed0, landed1, landedf, mix,
    load_sem, send1, recv1, send2, recv2, own_sem, edge_send, edge_recv,
):
    comb, pool, outgoing = (comb0, comb1), (pool0, pool1), (outgoing0, outgoing1)
    rim, pack, landed = (e0, e1), (pack0, pack1), (landed0, landed1)
    n = lax.axis_size("member")
    nlat = lax.axis_size("lat")
    me = lax.axis_index("member")
    lat = lax.axis_index("lat")
    across = 1 - lax.axis_index("lon")
    up = lax.rem(lat + nlat - 1, nlat)
    down = lax.rem(lat + 1, nlat)

    loads = [pltpu.make_async_copy(state.at[:, :, k], comb[k].at[0:2], load_sem.at[k]) for k in range(2)]
    loads.append(pltpu.make_async_copy(forcing_hbm, forcing, load_sem.at[2]))
    loads.append(pltpu.make_async_copy(kick_hbm, kick, load_sem.at[3]))
    for load in loads:
        load.start()

    barrier = pltpu.get_barrier_semaphore()

    def greet(r, _):
        pl.semaphore_signal(barrier, 1, device_id={"member": lax.rem(me + r, n)}, device_id_type=MESH)
        return 0

    lax.fori_loop(1, n, greet, 0)
    for peer in (
        {"lat": up}, {"lat": down}, {"lon": across},
        {"lat": up, "lon": across}, {"lat": down, "lon": across},
    ):
        pl.semaphore_signal(barrier, 1, device_id=peer, device_id_type=MESH)
    loads[0].wait()
    loads[1].wait()
    if nsrc == 1:
        first = tab[me] == 0

        def pick_one(v, c):
            for k in range(2):
                picked[0, v, k] = jnp.where(first, comb[k][0, v], comb[k][1, v])
            return c

        lax.fori_loop(0, 5, pick_one, 0)
    pl.semaphore_wait(barrier, n - 1 + 5)

    def window(piece):
        rows = pl.ds(pl.multiple_of(piece // 4 * 8, 8), 8)
        cols = pl.ds(pl.multiple_of(lax.rem(piece, 4) * 128, 128), 128)
        return rows, cols

    def given(k, rows, cols):
        if nsrc == 1:
            return picked.at[:, :, k, rows, cols]
        return comb[k].at[0:2, :, rows, cols]

    def spread(k, r):
        peer = lax.rem(me + r, n)
        return pltpu.make_async_remote_copy(
            given(k, *window(peer)), pool[k].at[me],
            send1.at[k, r], recv1.at[k, r], device_id={"member": peer}, device_id_type=MESH,
        )

    my_rows, my_cols = window(me)

    def collect(k, r):
        peer = lax.rem(me + r, n)
        return pltpu.make_async_remote_copy(
            outgoing[k].at[peer], comb[k].at[2 : 2 + ndst, :, my_rows, my_cols],
            send2.at[k, r], recv2.at[k, r], device_id={"member": peer}, device_id_type=MESH,
        )

    def peers(action):
        lax.fori_loop(1, n, lambda r, c: (action(r), c)[1], 0)

    for k in range(2):
        peers(lambda r: spread(k, r).start())
    owns = [pltpu.make_async_copy(given(k, my_rows, my_cols), pool[k].at[me], own_sem.at[k]) for k in range(2)]
    for own in owns:
        own.start()

    lane = lax.broadcasted_iota(jnp.int32, (32, 128), 1)

    def edge_copies(source, packed, arrived, base):
        hops = (
            (source.at[:, :, 8:16], source.at[:, :, 40:48], {"lat": up}),
            (source.at[:, :, 32:40], source.at[:, :, 0:8], {"lat": down}),
            (packed, arrived.at[:, 8:40], {"lon": across}),
            (packed.at[:, 0:8], arrived.at[:, 40:48], {"lat": up, "lon": across}),
            (packed.at[:, 24:32], arrived.at[:, 0:8], {"lat": down, "lon": across}),
        )
        return [
            pltpu.make_async_remote_copy(
                a, b, edge_send.at[base + i], edge_recv.at[base + i], device_id=peer, device_id_type=MESH
            )
            for i, (a, b, peer) in enumerate(hops)
        ]

    def lay_out(p, tiles, target, packed):
        target[p, 0, 8:40] = roll(tiles[0], 8)
        for c in range(1, 4):
            target[p, c, 8:40] = jnp.where(
                lane < 8 + 16 * c, roll(tiles[c - 1], 8 + 16 * c), roll(tiles[c], 8 + 16 * c)
            )
        target[p, 4, 8:40] = roll(tiles[3], 72)
        slot = lax.rem(p, 8)
        tile = roll(jnp.where(lane < 64, tiles[0], tiles[3]), 16 * slot)
        ours = lax.rem(lane + 8 + 128 - 16 * slot, 128) < 16
        packed[p // 8] = jnp.where(ours, tile, packed[p // 8])

    lane_tall = lax.broadcasted_iota(jnp.int32, (48, 128), 1)

    def add_columns(target, arrived):
        def one(p, c):
            turn = 128 - 16 * lax.rem(p, 8)
            source = arrived[p // 8]
            target[p, 0] = jnp.where(lane_tall < 8, roll(source, lax.rem(turn + 8, 128)), target[p, 0])
            target[p, 4] = jnp.where(lane_tall >= 72, roll(source, lax.rem(turn + 72, 128)), target[p, 4])
            return c

        lax.fori_loop(0, 10, one, 0)

    def clear_outside(target):
        @pl.when(lat == 0)
        def _():
            target[:, :, 0:8] = jnp.zeros((10, 5, 8, 128), jnp.float32)

        @pl.when(lat == nlat - 1)
        def _():
            target[:, :, 40:48] = jnp.zeros((10, 5, 8, 128), jnp.float32)

    def columns(ref, *index):
        return [ref[index + (slice(None), slice(t * 128, t * 128 + 128))] for t in range(4)]

    for k in range(2):
        pack[k][...] = jnp.zeros(pack[k].shape, jnp.float32)
    packf[...] = jnp.zeros(packf.shape, jnp.float32)
    loads[2].wait()

    def lay_forcing(p, c):
        tiles = columns(forcing, lax.rem(p, 5), p // 5)
        lay_out(p, [0.1 * t for t in tiles], f_ref, packf)
        return c

    lax.fori_loop(0, 10, lay_forcing, 0)
    f_copies = edge_copies(f_ref, packf, landedf, 10)
    for copy in f_copies:
        copy.start()

    for k in range(2):
        for v in range(5):
            table = coupling[v]
            for w in range(5):
                scaled = 0.25 * table[k, w]
                mix[k, v, w] = scaled + 0.75 if v == w else scaled

    for k in range(2):
        owns[k].wait()
        peers(lambda r: spread(k, r).wait_recv())

        def choose(d, c):
            for j in range(ndst):
                source = clone[2 * d + j] if ndst == 2 else clone[2 * d + tab[16 + d]]
                place = lax.rem(source, 2) if nsrc == 2 else 0
                outgoing[k][d, j] = pool[k][source // 2, place]
            return c

        lax.fori_loop(0, n, choose, 0)
        peers(lambda r: collect(k, r).start())
        mine = pltpu.make_async_copy(
            outgoing[k].at[me], comb[k].at[2 : 2 + ndst, :, my_rows, my_cols], own_sem.at[k]
        )
        mine.start()
        owns[k] = mine

    loads[3].wait()
    for k in range(2):
        peers(lambda r: spread(k, r).wait_send())
    for copy in f_copies:
        copy.wait()
    add_columns(f_ref, landedf)

    row_at = lax.broadcasted_iota(jnp.int32, (8, 128), 0)
    low = jnp.where(lat == 0, HALO, 0)
    high = jnp.where(lat == nlat - 1, 40, 48)
    near, far, first, second = 0.8 / 12.0, 0.05 / 12.0, 0.4 / 12.0, 0.05 / 12.0

    def sweep(k, source, target, starts):
        def tile(it, carry):
            m, c = it // 5, lax.rem(it, 5)
            for row in starts:
                centre = [source[5 * m + v, c, row : row + 8] for v in range(5)]
                u1, v1 = centre[0] * first, centre[1] * first
                u2, v2 = centre[0] * second, centre[1] * second
                ce1, cw1, ce2, cw2 = near - u1, near + u1, u2 - far, -far - u2
                cs1, cn1, cs2, cn2 = near - v1, near + v1, v2 - far, -far - v2
                for v in range(5):
                    p = 5 * m + v
                    here = centre[v]
                    along = cw1 * roll(here, 1) + ce1 * roll(here, -1)
                    along = along + (cw2 * roll(here, 2) + ce2 * roll(here, -2))
                    cross = cn1 * source[p, c, row - 1 : row + 7] + cs1 * source[p, c, row + 1 : row + 9]
                    cross = cross + (
                        cn2 * source[p, c, row - 2 : row + 6] + cs2 * source[p, c, row + 2 : row + 10]
                    )
                    rest = f_ref[5 * k + v, c, row : row + 8] + mix[k, v, 0] * centre[0]
                    for q in range(1, 5):
                        rest = rest + mix[k, v, q] * centre[q]
                    total = (along + cross) + rest
                    if row < 8 or row > 32:
                        inside = (row_at + row >= low) & (row_at + row < high)
                        total = jnp.where(inside, total, 0.0)
                    target[p, c, row : row + 8] = total
            return carry

        lax.fori_loop(0, 10, tile, 0)

    for k in range(2):
        owns[k].wait()
        peers(lambda r: collect(k, r).wait_recv())

        def begin(p, c):
            m, v = p // 5, lax.rem(p, 5)
            source = clone[2 * me + m]
            other = 2 + m if ndst == 2 else 2
            pick = jnp.where(source // 2 == me, lax.rem(source, 2), other)
            taken = columns(comb[k], pick, v)
            kicks = columns(kick, m, v, k)
            lay_out(p, [a + b for a, b in zip(taken, kicks)], rim[k], pack[k])
            return c

        lax.fori_loop(0, 10, begin, 0)
        copies = edge_copies(rim[k], pack[k], landed[k], 5 * k)
        for copy in copies:
            copy.start()
        for copy in copies:
            copy.wait()
        add_columns(rim[k], landed[k])
        clear_outside(rim[k])
        sweep(k, rim[k], work_a, (2, 10, 18, 26, 34, 38))
        sweep(k, work_a, work_b, (4, 12, 20, 28, 36))
        sweep(k, work_b, work_a, (6, 14, 22, 30, 34))
        sweep(k, work_a, work_b, (8, 16, 24, 32))

        def finish(p, c):
            m, v = p // 5, lax.rem(p, 5)
            turned = [roll(work_b[p, t, 8:40], -8 - 16 * t) for t in range(5)]
            for t in range(4):
                out_ref[m, v, k, :, t * 128 : t * 128 + 128] = jnp.where(
                    lane < WIDE - 16 * t, turned[t], turned[t + 1]
                )
            return c

        lax.fori_loop(0, 10, finish, 0)

    for k in range(2):
        peers(lambda r: collect(k, r).wait_send())


def run(nsrc, ndst, tab, clone_src, state, kick, forcing, coupling):
    n = lax.axis_size("member")
    f32 = jnp.float32
    vmem = pl.BlockSpec(memory_space=pltpu.VMEM)
    smem = pl.BlockSpec(memory_space=pltpu.SMEM)
    hbm = pl.BlockSpec(memory_space=pl.ANY)
    dma = pltpu.SemaphoreType.DMA
    member = state.shape[1:]
    level = (member[0],) + member[2:]
    padded = pltpu.VMEM((10, 5, 48, 128), f32)
    packed = pltpu.VMEM((2, 32, 128), f32)
    arrived = pltpu.VMEM((2, 48, 128), f32)
    return pl.pallas_call(
        functools.partial(kernel, nsrc, ndst),
        out_shape=jax.ShapeDtypeStruct(state.shape, f32),
        in_specs=[smem, smem, hbm, hbm, hbm, vmem],
        out_specs=vmem,
        scratch_shapes=[
            pltpu.VMEM((2 + ndst,) + level, f32), pltpu.VMEM((2 + ndst,) + level, f32),
            pltpu.VMEM(state.shape, f32), pltpu.VMEM(member, f32), pltpu.VMEM((1,) + member, f32),
            pltpu.VMEM((n, nsrc, 5, 8, 128), f32), pltpu.VMEM((n, nsrc, 5, 8, 128), f32),
            pltpu.VMEM((n, ndst, 5, 8, 128), f32), pltpu.VMEM((n, ndst, 5, 8, 128), f32),
            padded, padded, padded, padded, padded,
            packed, packed, packed, arrived, arrived, arrived,
            pltpu.SMEM((2, 5, 5), f32),
            dma((4,)), dma((2, n)), dma((2, n)), dma((2, n)), dma((2, n)),
            dma((2,)), dma((15,)), dma((15,)),
        ],
        compiler_params=pltpu.CompilerParams(collective_id=2 * nsrc + ndst, has_side_effects=True),
        name=f"advance_{nsrc}_{ndst}",
    )(tab, clone_src, state, kick, forcing, coupling.transpose(1, 0, 2))


def plan_kernel(clone, tab, wanted):
    def clear(m, c):
        wanted[m] = 0
        return c

    lax.fori_loop(0, 32, clear, 0)

    def mark(m, c):
        source = clone[m]

        @pl.when(jnp.right_shift(source, 1) != jnp.right_shift(m, 1))
        def _():
            wanted[source] = 1

        return c

    lax.fori_loop(0, 32, mark, 0)

    def count(d, most):
        gives, takes = most
        tab[d] = jnp.where(wanted[2 * d] == 1, 0, 1)
        gives = jnp.maximum(gives, wanted[2 * d] + wanted[2 * d + 1] - 1)
        one, two = clone[2 * d], clone[2 * d + 1]
        far_one = jnp.right_shift(one, 1) != d
        far_two = jnp.right_shift(two, 1) != d
        tab[16 + d] = jnp.where(far_one, 0, 1)
        both = far_one & far_two & (one != two)
        return gives, jnp.maximum(takes, jnp.where(both, 1, 0))

    gives, takes = lax.fori_loop(0, 16, count, (jnp.int32(0), jnp.int32(0)))
    tab[32] = 2 * gives + takes


def shards(state, kick, forcing, coupling, clone_src):
    smem = pl.BlockSpec(memory_space=pltpu.SMEM)
    tab = pl.pallas_call(
        plan_kernel,
        out_shape=jax.ShapeDtypeStruct((33,), jnp.int32),
        in_specs=[smem],
        out_specs=smem,
        scratch_shapes=[pltpu.SMEM((32,), jnp.int32)],
        name="plan",
    )(clone_src)
    cases = [functools.partial(run, nsrc, ndst) for nsrc in (1, 2) for ndst in (1, 2)]
    return lax.switch(tab[32], cases, tab, clone_src, state, kick, forcing, coupling)


def solution(mesh):
    block = P("member", None, None, "lat", "lon")
    in_specs = (block, block, P(None, None, "lat", "lon"), P(), P())
    return jax.shard_map(shards, mesh=mesh, in_specs=in_specs, out_specs=block, check_vma=False)
```

```python
import functools

import jax
import jax.numpy as jnp
from jax import lax
from jax.experimental import pallas as pl
from jax.experimental.pallas import tpu as pltpu
from jax.sharding import PartitionSpec as P

HALO = 8
WIDE = 112
MESH = pl.DeviceIdType.MESH


def roll(values, shift):
    if isinstance(shift, int):
        shift = shift % 128
    return pltpu.roll(values, shift, axis=values.ndim - 1)


def kernel(
    nsrc, ndst, tab, clone, state, kick_hbm, forcing_hbm, coupling, out_ref,
    comb0, comb1, kick, forcing, picked, pool0, pool1, outgoing0, outgoing1,
    e0, e1, f_ref, work_a, work_b, pack0, pack1, packf, landed0, landed1, landedf, mix, shift,
    load_sem, send1, recv1, send2, recv2, own_sem, edge_send, edge_recv,
):
    comb, pool, outgoing = (comb0, comb1), (pool0, pool1), (outgoing0, outgoing1)
    rim, pack, landed = (e0, e1), (pack0, pack1), (landed0, landed1)
    n = lax.axis_size("member")
    nlat = lax.axis_size("lat")
    me = lax.axis_index("member")
    lat = lax.axis_index("lat")
    across = 1 - lax.axis_index("lon")
    up = lax.rem(lat + nlat - 1, nlat)
    down = lax.rem(lat + 1, nlat)

    loads = [pltpu.make_async_copy(state.at[:, :, k], comb[k].at[0:2], load_sem.at[k]) for k in range(2)]
    loads.append(pltpu.make_async_copy(forcing_hbm, forcing, load_sem.at[2]))
    loads.append(pltpu.make_async_copy(kick_hbm, kick, load_sem.at[3]))
    for load in loads:
        load.start()

    barrier = pltpu.get_barrier_semaphore()

    def greet(r, _):
        pl.semaphore_signal(barrier, 1, device_id={"member": lax.rem(me + r, n)}, device_id_type=MESH)
        return 0

    lax.fori_loop(1, n, greet, 0)
    for peer in (
        {"lat": up}, {"lat": down}, {"lon": across},
        {"lat": up, "lon": across}, {"lat": down, "lon": across},
    ):
        pl.semaphore_signal(barrier, 1, device_id=peer, device_id_type=MESH)
    loads[0].wait()
    loads[1].wait()
    if nsrc == 1:
        first = tab[me] == 0

        def pick_one(v, c):
            for k in range(2):
                picked[0, v, k] = jnp.where(first, comb[k][0, v], comb[k][1, v])
            return c

        lax.fori_loop(0, 5, pick_one, 0)
    pl.semaphore_wait(barrier, n - 1 + 5)

    def window(piece):
        rows = pl.ds(pl.multiple_of(piece // 4 * 8, 8), 8)
        cols = pl.ds(pl.multiple_of(lax.rem(piece, 4) * 128, 128), 128)
        return rows, cols

    def given(k, rows, cols):
        if nsrc == 1:
            return picked.at[:, :, k, rows, cols]
        return comb[k].at[0:2, :, rows, cols]

    def spread(k, r):
        peer = lax.rem(me + r, n)
        return pltpu.make_async_remote_copy(
            given(k, *window(peer)), pool[k].at[me],
            send1.at[k, r], recv1.at[k, r], device_id={"member": peer}, device_id_type=MESH,
        )

    my_rows, my_cols = window(me)

    def collect(k, r):
        peer = lax.rem(me + r, n)
        return pltpu.make_async_remote_copy(
            outgoing[k].at[peer], comb[k].at[2 : 2 + ndst, :, my_rows, my_cols],
            send2.at[k, r], recv2.at[k, r], device_id={"member": peer}, device_id_type=MESH,
        )

    def peers(action):
        lax.fori_loop(1, n, lambda r, c: (action(r), c)[1], 0)

    for k in range(2):
        peers(lambda r: spread(k, r).start())
    owns = [pltpu.make_async_copy(given(k, my_rows, my_cols), pool[k].at[me], own_sem.at[k]) for k in range(2)]
    for own in owns:
        own.start()

    lane = lax.broadcasted_iota(jnp.int32, (32, 128), 1)

    def edge_copies(source, packed, arrived, base):
        hops = (
            (source.at[:, :, 8:16], source.at[:, :, 40:48], {"lat": up}),
            (source.at[:, :, 32:40], source.at[:, :, 0:8], {"lat": down}),
            (packed, arrived.at[:, 8:40], {"lon": across}),
            (packed.at[:, 0:8], arrived.at[:, 40:48], {"lat": up, "lon": across}),
            (packed.at[:, 24:32], arrived.at[:, 0:8], {"lat": down, "lon": across}),
        )
        return [
            pltpu.make_async_remote_copy(
                a, b, edge_send.at[base + i], edge_recv.at[base + i], device_id=peer, device_id_type=MESH
            )
            for i, (a, b, peer) in enumerate(hops)
        ]

    def lay_out(p, tiles, target, packed):
        target[p, 0, 8:40] = roll(tiles[0], 8)
        for c in range(1, 4):
            target[p, c, 8:40] = jnp.where(
                lane < 8 + 16 * c, roll(tiles[c - 1], 8 + 16 * c), roll(tiles[c], 8 + 16 * c)
            )
        target[p, 4, 8:40] = roll(tiles[3], 72)
        slot = lax.rem(p, 8)
        tile = roll(jnp.where(lane < 64, tiles[0], tiles[3]), 16 * slot)
        ours = lax.rem(lane + 8 + 128 - 16 * slot, 128) < 16
        packed[p // 8] = jnp.where(ours, tile, packed[p // 8])

    lane_tall = lax.broadcasted_iota(jnp.int32, (48, 128), 1)

    def add_columns(target, arrived):
        def one(p, c):
            turn = 128 - 16 * lax.rem(p, 8)
            source = arrived[p // 8]
            target[p, 0] = jnp.where(lane_tall < 8, roll(source, lax.rem(turn + 8, 128)), target[p, 0])
            target[p, 4] = jnp.where(lane_tall >= 72, roll(source, lax.rem(turn + 72, 128)), target[p, 4])
            return c

        lax.fori_loop(0, 10, one, 0)

    def clear_outside(target):
        @pl.when(lat == 0)
        def _():
            target[:, :, 0:8] = jnp.zeros((10, 5, 8, 128), jnp.float32)

        @pl.when(lat == nlat - 1)
        def _():
            target[:, :, 40:48] = jnp.zeros((10, 5, 8, 128), jnp.float32)

    def columns(ref, *index):
        return [ref[index + (slice(None), slice(t * 128, t * 128 + 128))] for t in range(4)]

    for k in range(2):
        pack[k][...] = jnp.zeros(pack[k].shape, jnp.float32)
    packf[...] = jnp.zeros(packf.shape, jnp.float32)
    loads[2].wait()

    def lay_forcing(p, c):
        tiles = columns(forcing, lax.rem(p, 5), p // 5)
        lay_out(p, [0.1 * t for t in tiles], f_ref, packf)
        return c

    lax.fori_loop(0, 10, lay_forcing, 0)
    f_copies = edge_copies(f_ref, packf, landedf, 10)
    for copy in f_copies:
        copy.start()

    for k in range(2):
        for v in range(5):
            table = coupling[v]
            for w in range(5):
                scaled = 0.25 * table[k, w]
                mix[k, v, w] = scaled + 0.75 if v == w else scaled

    row_in = lax.broadcasted_iota(jnp.int32, (256, 256), 0)
    col_out = lax.broadcasted_iota(jnp.int32, (256, 256), 1)
    step = jnp.bitwise_and(row_in - col_out + 256, 127)
    one, two = jnp.where(step == 1, 1.0, 0.0), jnp.where(step == 2, 1.0, 0.0)
    back_one, back_two = jnp.where(step == 127, 1.0, 0.0), jnp.where(step == 126, 1.0, 0.0)
    slope = 8.0 * (one - back_one) - (two - back_two)
    spread_out = 16.0 * (one + back_one) - (two + back_two)
    shift[...] = jnp.where(col_out < 128, slope, spread_out).astype(jnp.bfloat16)

    for k in range(2):
        owns[k].wait()
        peers(lambda r: spread(k, r).wait_recv())

        def choose(d, c):
            for j in range(ndst):
                source = clone[2 * d + j] if ndst == 2 else clone[2 * d + tab[16 + d]]
                place = lax.rem(source, 2) if nsrc == 2 else 0
                outgoing[k][d, j] = pool[k][source // 2, place]
            return c

        lax.fori_loop(0, n, choose, 0)
        peers(lambda r: collect(k, r).start())
        mine = pltpu.make_async_copy(
            outgoing[k].at[me], comb[k].at[2 : 2 + ndst, :, my_rows, my_cols], own_sem.at[k]
        )
        mine.start()
        owns[k] = mine

    loads[3].wait()
    for k in range(2):
        peers(lambda r: spread(k, r).wait_send())
    for copy in f_copies:
        copy.wait()
    add_columns(f_ref, landedf)

    row_at = lax.broadcasted_iota(jnp.int32, (8, 128), 0)
    low = jnp.where(lat == 0, HALO, 0)
    high = jnp.where(lat == nlat - 1, 40, 48)
    near, far, first, second = 0.8 / 12.0, 0.05 / 12.0, 0.4 / 12.0, 0.05 / 12.0

    def sweep(k, source, target, starts):
        def tile(it, carry):
            m, c = it // 5, lax.rem(it, 5)
            field = jnp.concatenate(
                [source[5 * m + v, c, row : row + 8] for row in starts for v in range(5)], axis=0
            )
            coarse = field.astype(jnp.bfloat16)
            fine = (field - coarse.astype(jnp.float32)).astype(jnp.bfloat16)
            lonwise = jnp.dot(
                jnp.concatenate([coarse, fine], axis=1), shift[...], preferred_element_type=jnp.float32
            )
            for i, row in enumerate(starts):
                centre = [source[5 * m + v, c, row : row + 8] for v in range(5)]
                u2 = centre[0] * second
                v1, v2 = centre[1] * first, centre[1] * second
                cs1, cn1, cs2, cn2 = near - v1, near + v1, v2 - far, -far - v2
                for v in range(5):
                    p = 5 * m + v
                    at = 8 * (5 * i + v)
                    along = far * lonwise[at : at + 8, 128:256] - u2 * lonwise[at : at + 8, 0:128]
                    cross = cn1 * source[p, c, row - 1 : row + 7] + cs1 * source[p, c, row + 1 : row + 9]
                    cross = cross + (
                        cn2 * source[p, c, row - 2 : row + 6] + cs2 * source[p, c, row + 2 : row + 10]
                    )
                    rest = f_ref[5 * k + v, c, row : row + 8] + mix[k, v, 0] * centre[0]
                    for q in range(1, 5):
                        rest = rest + mix[k, v, q] * centre[q]
                    total = (along + cross) + rest
                    if row < 8 or row > 32:
                        inside = (row_at + row >= low) & (row_at + row < high)
                        total = jnp.where(inside, total, 0.0)
                    target[p, c, row : row + 8] = total
            return carry

        lax.fori_loop(0, 10, tile, 0)

    for k in range(2):
        owns[k].wait()
        peers(lambda r: collect(k, r).wait_recv())

        def begin(p, c):
            m, v = p // 5, lax.rem(p, 5)
            source = clone[2 * me + m]
            other = 2 + m if ndst == 2 else 2
            pick = jnp.where(source // 2 == me, lax.rem(source, 2), other)
            taken = columns(comb[k], pick, v)
            kicks = columns(kick, m, v, k)
            lay_out(p, [a + b for a, b in zip(taken, kicks)], rim[k], pack[k])
            return c

        lax.fori_loop(0, 10, begin, 0)
        copies = edge_copies(rim[k], pack[k], landed[k], 5 * k)
        for copy in copies:
            copy.start()
        for copy in copies:
            copy.wait()
        add_columns(rim[k], landed[k])
        clear_outside(rim[k])
        sweep(k, rim[k], work_a, (2, 10, 18, 26, 34, 38))
        sweep(k, work_a, work_b, (4, 12, 20, 28, 36))
        sweep(k, work_b, work_a, (6, 14, 22, 30, 34))
        sweep(k, work_a, work_b, (8, 16, 24, 32))

        def finish(p, c):
            m, v = p // 5, lax.rem(p, 5)
            turned = [roll(work_b[p, t, 8:40], -8 - 16 * t) for t in range(5)]
            for t in range(4):
                out_ref[m, v, k, :, t * 128 : t * 128 + 128] = jnp.where(
                    lane < WIDE - 16 * t, turned[t], turned[t + 1]
                )
            return c

        lax.fori_loop(0, 10, finish, 0)

    for k in range(2):
        peers(lambda r: collect(k, r).wait_send())


def run(nsrc, ndst, tab, clone_src, state, kick, forcing, coupling):
    n = lax.axis_size("member")
    f32 = jnp.float32
    vmem = pl.BlockSpec(memory_space=pltpu.VMEM)
    smem = pl.BlockSpec(memory_space=pltpu.SMEM)
    hbm = pl.BlockSpec(memory_space=pl.ANY)
    dma = pltpu.SemaphoreType.DMA
    member = state.shape[1:]
    level = (member[0],) + member[2:]
    padded = pltpu.VMEM((10, 5, 48, 128), f32)
    packed = pltpu.VMEM((2, 32, 128), f32)
    arrived = pltpu.VMEM((2, 48, 128), f32)
    return pl.pallas_call(
        functools.partial(kernel, nsrc, ndst),
        out_shape=jax.ShapeDtypeStruct(state.shape, f32),
        in_specs=[smem, smem, hbm, hbm, hbm, vmem],
        out_specs=vmem,
        scratch_shapes=[
            pltpu.VMEM((2 + ndst,) + level, f32), pltpu.VMEM((2 + ndst,) + level, f32),
            pltpu.VMEM(state.shape, f32), pltpu.VMEM(member, f32), pltpu.VMEM((1,) + member, f32),
            pltpu.VMEM((n, nsrc, 5, 8, 128), f32), pltpu.VMEM((n, nsrc, 5, 8, 128), f32),
            pltpu.VMEM((n, ndst, 5, 8, 128), f32), pltpu.VMEM((n, ndst, 5, 8, 128), f32),
            padded, padded, padded, padded, padded,
            packed, packed, packed, arrived, arrived, arrived,
            pltpu.SMEM((2, 5, 5), f32), pltpu.VMEM((256, 256), jnp.bfloat16),
            dma((4,)), dma((2, n)), dma((2, n)), dma((2, n)), dma((2, n)),
            dma((2,)), dma((15,)), dma((15,)),
        ],
        compiler_params=pltpu.CompilerParams(collective_id=2 * nsrc + ndst, has_side_effects=True),
        name=f"advance_{nsrc}_{ndst}",
    )(tab, clone_src, state, kick, forcing, coupling.transpose(1, 0, 2))


def plan_kernel(clone, tab, wanted):
    def clear(m, c):
        wanted[m] = 0
        return c

    lax.fori_loop(0, 32, clear, 0)

    def mark(m, c):
        source = clone[m]

        @pl.when(jnp.right_shift(source, 1) != jnp.right_shift(m, 1))
        def _():
            wanted[source] = 1

        return c

    lax.fori_loop(0, 32, mark, 0)

    def count(d, most):
        gives, takes = most
        tab[d] = jnp.where(wanted[2 * d] == 1, 0, 1)
        gives = jnp.maximum(gives, wanted[2 * d] + wanted[2 * d + 1] - 1)
        one, two = clone[2 * d], clone[2 * d + 1]
        far_one = jnp.right_shift(one, 1) != d
        far_two = jnp.right_shift(two, 1) != d
        tab[16 + d] = jnp.where(far_one, 0, 1)
        both = far_one & far_two & (one != two)
        return gives, jnp.maximum(takes, jnp.where(both, 1, 0))

    gives, takes = lax.fori_loop(0, 16, count, (jnp.int32(0), jnp.int32(0)))
    tab[32] = 2 * gives + takes


def shards(state, kick, forcing, coupling, clone_src):
    smem = pl.BlockSpec(memory_space=pltpu.SMEM)
    tab = pl.pallas_call(
        plan_kernel,
        out_shape=jax.ShapeDtypeStruct((33,), jnp.int32),
        in_specs=[smem],
        out_specs=smem,
        scratch_shapes=[pltpu.SMEM((32,), jnp.int32)],
        name="plan",
    )(clone_src)
    cases = [functools.partial(run, nsrc, ndst) for nsrc in (1, 2) for ndst in (1, 2)]
    return lax.switch(tab[32], cases, tab, clone_src, state, kick, forcing, coupling)


def solution(mesh):
    block = P("member", None, None, "lat", "lon")
    in_specs = (block, block, P(None, None, "lat", "lon"), P(), P())
    return jax.shard_map(shards, mesh=mesh, in_specs=in_specs, out_specs=block, check_vma=False)
```
